256 devices in a mesh: pipe: 8 (over y, core), expert: 32 (over x, z).
Axes of the slice: x: 4, y: 4, z: 8, core: 2. Of those that a mesh axis runs over, the one named last changes fastest.
Arguments:
- state: bfloat16 [8, 1536, 2048], P('pipe', 'expert'), may hold values from -6 to 6
- route_ids: int32 [3, 8, 1536, 8], P(None, 'pipe', 'expert'), may hold values from 0 to 31, all different within a row; in each aligned block of 48 rows (0 to 47, 48 to 95, ..., all dimensions but the last counted through in order) at most 16 rows name the same one
- route_weights: float32 [3, 8, 1536, 8], P(None, 'pipe', 'expert'), may hold values from 0.02 to 0.3
- norm_gain: float32 [8, 2048], P('pipe'), may hold values from 0.1 to 1.9
- w_gate: bfloat16 [8, 32, 2048, 768], P('pipe', 'expert'), may hold values from -0.125 to 0.125
- w_up: bfloat16 [8, 32, 2048, 768], P('pipe', 'expert'), may hold values from -0.125 to 0.125
- w_down: bfloat16 [8, 32, 768, 2048], P('pipe', 'expert'), may hold values from -0.21875 to 0.21875
Outputs:
- final_state: bfloat16 [8, 1536, 2048], P('pipe', 'expert')
The draws below stay inside these ranges and needn't reach their ends.
Inputs may be any that keep to these rules, and one draw needn't show every extreme that they name: `route_ids`: each token names 8 different experts. In the routes of one device (a block of 48 tokens of one step and section) no expert is named more than 16 times, and in every draw some block names an expert exactly 16 times.
All inputs are finite; a program needn't handle non-finite values.
Results may differ from the reference program's by a relative error of at most 0.0065.
Values may be sent and summed in bfloat16 or wider, within the bound.
No kernel may reach another device: no remote copies, remote signals or barrier semaphores. Data moves between devices by JAX's collectives and lax.ppermute only.
A program may use at most 64 MiB of HBM per device.

```python
import math
import jax
import jax.numpy as jnp
import numpy as np
from jax import lax

D = 2048
FF = 768
TOP = 8
PANEL = 48
TICKS = 3
SECTIONS = 8
EXPERTS = 32
TOK = 1536
MOST = 16
N_EXPERT = 32


def shard_levels(own_key, extent, pieces, low, high):
    loudness, own = 1.0, jax.random.fold_in(own_key, 6)
    for axis_at, blocks in pieces:
        draws = jnp.exp(jax.random.uniform(jax.random.fold_in(own, axis_at), (blocks,), jnp.float32, low / len(pieces), high / len(pieces)))
        loudness = loudness * jnp.repeat(draws, extent[axis_at] // blocks).reshape([-1 if axis == axis_at else 1 for axis in range(len(extent))])
    return loudness


def shared_out(key, own, number, rows, amount, top, bound, lean):
    order = jax.random.permutation(key, amount)
    heavy_load, usual = load_shares(amount, rows * top, bound, lean, True), load_shares(amount, rows * top, bound, lean, False)
    places = jnp.arange(amount)

    def named(tallies, turn):
        used = int((tallies > 0).sum())
        fixed = max(1, used // 4)
        passed = fixed + (places - fixed + turn * (used - fixed)) % max(1, amount - fixed)
        return jnp.zeros((amount,), jnp.int32).at[order[jnp.where(places < fixed, places, passed)]].set(jnp.asarray(tallies, jnp.int32))

    tallies = jnp.where(number % 4 == 0, named(heavy_load, number // 4), named(usual, number - number // 4 - 1))
    mixed = jax.random.permutation(jax.random.fold_in(own, 3), amount)
    donor, sink = mixed[0:amount // 2 * 2:2], mixed[1:amount // 2 * 2:2]
    slack = jnp.minimum(tallies[donor] - 1, bound - tallies[sink]) // 2
    slack = jnp.where((donor == order[0]) | (sink == order[0]) | (tallies[sink] == 0), 0, jnp.maximum(slack, 0))
    passed = jax.random.randint(jax.random.fold_in(own, 4), (amount // 2,), 0, 1 << 20) % (slack + 1)
    tallies = tallies.at[donor].add(-passed).at[sink].add(passed)
    labels = jnp.searchsorted(jnp.cumsum(tallies), jnp.arange(rows * top), side="right").astype(jnp.int32)
    listing = labels.reshape(top, rows).T
    listing = listing[jax.random.permutation(jax.random.fold_in(own, 1), rows)]
    turn = jax.random.randint(jax.random.fold_in(own, 2), (rows, 1), 0, top)
    return jnp.take_along_axis(listing, (jnp.arange(top)[None, :] + turn) % top, axis=1)


def load_shares(amount, total, reach, lean, full):
    weights = [(1 << 20) // math.isqrt(rank ** lean) + 1 for rank in range(1, amount + 1)]
    largest = reach if full else min(reach, max(-(-total // amount), total * weights[0] // sum(weights)))
    least = 1 if total - largest >= amount - 1 else 0
    counts, spare = [largest] + [least] * (amount - 1), total - largest - least * (amount - 1)
    while spare > 0:
        candidates = [i for i in range(1, amount) if counts[i] < largest] or [i for i in range(1, amount) if counts[i] < reach]
        pool, remaining = sum([weights[i] for i in candidates]), spare
        for i in candidates:
            more = min(reach - counts[i], max(1, remaining * weights[i] // pool), spare)
            counts[i] = counts[i] + more
            spare = spare - more
    return np.array(counts)


def scatter_about(own_key, dims, spread, most, shards=(), kind=jnp.bfloat16):
    values = spread * jax.random.normal(own_key, dims, jnp.float32)
    if shards:
        values = values * shard_levels(own_key, dims, shards, -0.22, 0.18)
    return jnp.clip(values, -most, most).astype(kind)


def setup_inputs(seed: int = 0) -> dict:
    arg_keys = jax.random.split(jax.random.key(seed), 8)
    state = scatter_about(arg_keys[0], (SECTIONS, TOK, D), 1.0, 6.0, ((0, 8), (1, 32)))
    route_ids_keys = jax.random.split(jax.random.fold_in(arg_keys[1], 1), TICKS * SECTIONS * TOK // PANEL)
    route_ids_turns = jax.random.permutation(jax.random.fold_in(arg_keys[1], 3), TICKS * SECTIONS * TOK // PANEL)
    route_ids = jax.vmap(lambda own, number: shared_out(jax.random.fold_in(arg_keys[1], 2), own, number, PANEL, EXPERTS, TOP, MOST, 1))(route_ids_keys, route_ids_turns).reshape((TICKS, SECTIONS, TOK, TOP))
    route_weights = jnp.clip(jnp.exp(math.log(0.3) - 2.7080503 * jax.random.uniform(arg_keys[2], (TICKS, SECTIONS, TOK, TOP), jnp.float32) ** shard_levels(arg_keys[2], (TICKS, SECTIONS, TOK, TOP), ((1, 8), (2, 32)), -0.2, 0.2)), 0.02, 0.3)
    norm_gain = jnp.clip(1.0 + 0.18 * jax.random.normal(arg_keys[3], (SECTIONS, D), jnp.float32), 0.1, 1.9)
    w_gate = scatter_about(arg_keys[4], (SECTIONS, EXPERTS, D, FF), D ** -0.5, 0.125, ((0, 8), (1, 32)))
    w_up = scatter_about(arg_keys[5], (SECTIONS, EXPERTS, D, FF), D ** -0.5, 0.125, ((0, 8), (1, 32)))
    w_down = scatter_about(arg_keys[6], (SECTIONS, EXPERTS, FF, D), FF ** -0.5, 0.21875, ((0, 8), (1, 32)))
    return {"state": state, "route_ids": route_ids, "route_weights": route_weights, "norm_gain": norm_gain, "w_gate": w_gate, "w_up": w_up, "w_down": w_down}


def expert_ffn(rows, gate_weight, up_weight, down_weight):
    gate = jnp.dot(rows, gate_weight, preferred_element_type=jnp.float32)
    upper = jnp.dot(rows, up_weight, preferred_element_type=jnp.float32)
    hidden = (jax.nn.silu(gate) * upper).astype(jnp.bfloat16)
    return jnp.dot(hidden, down_weight, preferred_element_type=jnp.float32).astype(jnp.bfloat16)

def rms_scaled(panel, gain):
    widened = panel.astype(jnp.float32)
    scale = lax.rsqrt(lax.optimization_barrier(jnp.mean(widened * widened, axis=-1, keepdims=True)) + 1e-06)
    return (widened, (widened * scale * gain).astype(jnp.bfloat16))

def section_layer(panel, expert_ids, route_wts, gain, gate_weight, up_weight, down_weight):
    widened, normed = rms_scaled(panel, gain)
    matches = (expert_ids[:, :, None] == jnp.arange(EXPERTS, dtype=jnp.int32)).astype(jnp.int32)
    matches = matches.reshape(N_EXPERT, PANEL * TOP, EXPERTS)
    ranks = (jnp.cumsum(matches, axis=1) - 1).astype(jnp.int32)
    slot_of = lax.optimization_barrier(jnp.sum(ranks * matches, axis=2)).astype(jnp.int32)
    sources = jnp.arange(N_EXPERT, dtype=jnp.int32)[:, None]
    position = expert_ids.reshape(N_EXPERT, PANEL * TOP) * (N_EXPERT * MOST) + sources * MOST + slot_of
    position = position.reshape(-1).astype(jnp.int32)
    token_of = (jnp.arange(TOK * TOP, dtype=jnp.int32) // TOP).astype(jnp.int32)
    slot_token = jnp.zeros((EXPERTS * N_EXPERT * MOST,), jnp.int32).at[position].set(token_of)
    filled = jnp.zeros((EXPERTS * N_EXPERT * MOST,), jnp.int32).at[position].set(1)
    outgoing = jnp.where(filled[:, None] > 0, normed[slot_token], jnp.zeros((), jnp.bfloat16))
    outgoing = outgoing.reshape(EXPERTS, N_EXPERT * MOST, D)
    results = lax.map(lambda item: expert_ffn(item[0], item[1], item[2], item[3]), (outgoing, gate_weight, up_weight, down_weight))
    picked = results.reshape(-1, D)[position].reshape(TOK, TOP, D)
    combined = lax.optimization_barrier(jnp.sum(route_wts[:, :, None] * picked.astype(jnp.float32), axis=1))
    return (widened + combined).astype(jnp.bfloat16)

def reference(state, route_ids, route_weights, norm_gain, w_gate, w_up, w_down):
    panels = state
    for tick_index in range(TICKS):
        updated = lax.map(lambda item: section_layer(item[0], item[1], item[2], item[3], item[4], item[5], item[6]), (panels, route_ids[tick_index], route_weights[tick_index], norm_gain, w_gate, w_up, w_down))
        panels = jnp.roll(updated, 1, axis=0)
    return panels
```

```python
import functools

import jax
import jax.numpy as jnp
from jax import lax
from jax.experimental import pallas as pl
from jax.experimental.pallas import tpu as pltpu
from jax.sharding import PartitionSpec as P

F32 = jnp.float32
BF16 = jnp.bfloat16


def iota(shape, axis):
    return lax.broadcasted_iota(jnp.int32, shape, axis)


def table_kernel(experts, ids_ref, idst_ref, wts_ref, sel_ref, comb_ref):
    rows, chosen = ids_ref.shape[1], ids_ref.shape[2]
    places = sel_ref.shape[1]
    cap = places // experts
    hit_t = jnp.zeros((experts, rows), F32)
    hit = jnp.zeros((rows, experts), F32)
    weight = jnp.zeros((rows, experts), F32)
    for k in range(chosen):
        hit_t += (idst_ref[0, k : k + 1, :] == iota((experts, rows), 0)).astype(F32)
        here = ids_ref[0, :, k : k + 1] == iota((rows, experts), 1)
        hit += here.astype(F32)
        weight += jnp.where(here, wts_ref[0, :, k : k + 1], 0.0)
    before_t = (iota((rows, rows), 0) < iota((rows, rows), 1)).astype(BF16)
    before = (iota((rows, rows), 1) < iota((rows, rows), 0)).astype(BF16)
    rank_t = jnp.dot(hit_t.astype(BF16), before_t, preferred_element_type=F32)
    rank = jnp.dot(before, hit.astype(BF16), preferred_element_type=F32)
    code_t = jnp.where(hit_t > 0, rank_t, -1.0).astype(BF16)
    code = jnp.where(hit > 0, rank, -1.0).astype(BF16)
    high = weight.astype(BF16)
    low = (weight - high.astype(F32)).astype(BF16)
    spread_t = (iota((places, experts), 0) // cap == iota((places, experts), 1)).astype(BF16)
    spread = (iota((experts, places), 1) // cap == iota((experts, places), 0)).astype(BF16)
    slot_t = jnp.dot(spread_t, code_t, preferred_element_type=F32)
    slot = jnp.dot(code, spread, preferred_element_type=F32)
    want_t = (iota((places, rows), 0) % cap).astype(F32)
    want = (iota((rows, places), 1) % cap).astype(F32)
    sel_ref[0] = (slot_t == want_t).astype(BF16)
    for part, value in ((0, high), (1, low)):
        wide = jnp.dot(value, spread, preferred_element_type=F32)
        comb_ref[0, part * rows : (part + 1) * rows, :] = jnp.where(slot == want, wide, 0.0).astype(BF16)


def tables(ids, wts, experts, cap):
    ticks, rows, chosen = ids.shape
    places = experts * cap
    return pl.pallas_call(
        functools.partial(table_kernel, experts),
        grid=(ticks,),
        in_specs=[
            pl.BlockSpec((1, rows, chosen), lambda t: (t, 0, 0)),
            pl.BlockSpec((1, chosen, rows), lambda t: (t, 0, 0)),
            pl.BlockSpec((1, rows, chosen), lambda t: (t, 0, 0)),
        ],
        out_specs=[
            pl.BlockSpec((1, places, rows), lambda t: (t, 0, 0)),
            pl.BlockSpec((1, 2 * rows, places), lambda t: (t, 0, 0)),
        ],
        out_shape=[
            jax.ShapeDtypeStruct((ticks, places, rows), BF16),
            jax.ShapeDtypeStruct((ticks, 2 * rows, places), BF16),
        ],
        name="tables",
    )(ids, ids.transpose(0, 2, 1), wts)


def slot_kernel(x_ref, gain_ref, sel_ref, out_ref):
    wide = x_ref[...].astype(F32)
    scale = lax.rsqrt(jnp.mean(wide * wide, axis=-1, keepdims=True) + 1e-06)
    normed = (wide * scale * gain_ref[...]).astype(BF16)
    out_ref[...] = jnp.dot(sel_ref[...], normed, preferred_element_type=F32).astype(BF16)


def slotted(x, gain, sel):
    return pl.pallas_call(
        slot_kernel,
        out_shape=jax.ShapeDtypeStruct((sel.shape[0], x.shape[1]), BF16),
        name="slotted",
    )(x, gain, sel)


def ffn_kernel(x_ref, gate_ref, up_ref, down_ref, out_ref, acc_ref):
    step = pl.program_id(0)
    x = x_ref[...]
    gate = jnp.dot(x, gate_ref[...], preferred_element_type=F32)
    upper = jnp.dot(x, up_ref[...], preferred_element_type=F32)
    hidden = (gate / (1.0 + jnp.exp(-gate)) * upper).astype(BF16)
    part = jnp.dot(hidden, down_ref[...], preferred_element_type=F32)
    last = pl.num_programs(0) - 1

    @pl.when(step == 0)
    def _():
        acc_ref[...] = part

    @pl.when((step > 0) & (step < last))
    def _():
        acc_ref[...] += part

    @pl.when(step == last)
    def _():
        out_ref[...] = (acc_ref[...] + part).astype(BF16)


def ffn(x, gate, up, down):
    rows, width = x.shape
    hidden = gate.shape[1]
    block = 256
    return pl.pallas_call(
        ffn_kernel,
        grid=(hidden // block,),
        in_specs=[
            pl.BlockSpec((rows, width), lambda f: (0, 0)),
            pl.BlockSpec((width, block), lambda f: (0, f)),
            pl.BlockSpec((width, block), lambda f: (0, f)),
            pl.BlockSpec((block, width), lambda f: (f, 0)),
        ],
        out_specs=pl.BlockSpec((rows, width), lambda f: (0, 0)),
        out_shape=jax.ShapeDtypeStruct((rows, width), BF16),
        scratch_shapes=[pltpu.VMEM((rows, width), F32)],
        compiler_params=pltpu.CompilerParams(vmem_limit_bytes=48 << 20),
        cost_estimate=pl.CostEstimate(
            flops=6 * rows * width * hidden,
            bytes_accessed=6 * width * hidden + 4 * rows * width,
            transcendentals=rows * hidden,
        ),
        name="ffn",
    )(x, gate, up, down)


def combine_kernel(x_ref, back_ref, comb_ref, out_ref):
    rows = x_ref.shape[0]
    both = jnp.dot(comb_ref[...], back_ref[...], preferred_element_type=F32)
    out_ref[...] = (x_ref[...].astype(F32) + (both[:rows] + both[rows:])).astype(BF16)


def combined(x, back, comb):
    return pl.pallas_call(
        combine_kernel,
        out_shape=jax.ShapeDtypeStruct(x.shape, BF16),
        name="combined",
    )(x, back, comb)


def shards(state, route_ids, route_weights, norm_gain, w_gate, w_up, w_down):
    experts = lax.axis_size("expert")
    sections = lax.axis_size("pipe")
    panel = state[0]
    rows, width = panel.shape
    cap = 16
    sel, comb = tables(route_ids[:, 0], route_weights[:, 0], experts, cap)
    ring = [(i, (i + 1) % sections) for i in range(sections)]
    for tick in range(route_ids.shape[0]):
        outgoing = slotted(panel, norm_gain, sel[tick])
        incoming = lax.all_to_all(
            outgoing.reshape(experts, cap, width), "expert", split_axis=0, concat_axis=0, tiled=True
        )
        results = ffn(incoming.reshape(experts * cap, width), w_gate[0, 0], w_up[0, 0], w_down[0, 0])
        back = lax.all_to_all(
            results.reshape(experts, cap, width), "expert", split_axis=0, concat_axis=0, tiled=True
        )
        updated = combined(panel, back.reshape(experts * cap, width), comb[tick])
        panel = lax.ppermute(updated, "pipe", ring)
    return panel[None]


def solution(mesh):
    placed = (
        P("pipe", "expert", None),
        P(None, "pipe", "expert", None),
        P(None, "pipe", "expert", None),
        P("pipe", None),
        P("pipe", "expert", None, None),
        P("pipe", "expert", None, None),
        P("pipe", "expert", None, None),
    )
    return jax.shard_map(
        shards, mesh=mesh, in_specs=placed, out_specs=P("pipe", "expert", None), check_vma=False
    )
```

```python
import functools

import jax
import jax.numpy as jnp
from jax import lax
from jax.experimental import pallas as pl
from jax.experimental.pallas import tpu as pltpu
from jax.sharding import PartitionSpec as P

F32 = jnp.float32
BF16 = jnp.bfloat16
CAP = 16
RING = 8
GROUPS = ((0, 1, -1), (2, -2, 4), (3, -3))
ORDER = tuple(k for group in GROUPS for k in group)


def iota(shape, axis):
    return lax.broadcasted_iota(jnp.int32, shape, axis)


def route_kernel(ids_ref, wts_ref, out_ref):
    ticks, chosen, rows = ids_ref.shape
    experts = out_ref.shape[2]
    before = (iota((rows, rows), 0) < iota((rows, rows), 1)).astype(BF16)
    for t in range(ticks):
        hit = jnp.zeros((experts, rows), F32)
        weight = jnp.zeros((experts, rows), F32)
        for k in range(chosen):
            here = ids_ref[t, k : k + 1, :] == iota((experts, rows), 0)
            hit += here.astype(F32)
            weight += jnp.where(here, wts_ref[t, k : k + 1, :], 0.0)
        rank = jnp.dot(hit.astype(BF16), before, preferred_element_type=F32)
        out_ref[t, 0] = jnp.where(hit > 0, rank, -1.0)
        out_ref[t, 1] = weight


def routes(ids, wts, experts):
    ticks, rows, chosen = ids.shape
    return pl.pallas_call(
        route_kernel,
        out_shape=jax.ShapeDtypeStruct((ticks, 2, experts, rows), F32),
        name="routes",
    )(ids.transpose(0, 2, 1), wts.transpose(0, 2, 1))


def spread(table, columns, rows):
    return jnp.concatenate(
        [jnp.broadcast_to(table[j : j + 1, :], (CAP, rows)) for j in range(columns)], axis=0
    )


def select_kernel(tick, places, columns, table_ref, gain_ref, *refs):
    count = len(places)
    blocks, outs = refs[:count], refs[count:]
    rows = blocks[0].shape[0]
    base = tick * 2 * columns
    want = (iota((columns * CAP, rows), 0) % CAP).astype(F32)
    for n, place in enumerate(places):
        wide = blocks[n][...].astype(F32)
        scale = lax.rsqrt(jnp.mean(wide * wide, axis=-1, keepdims=True) + 1e-06)
        normed = (wide * scale * gain_ref[...]).astype(BF16)
        slot = spread(table_ref[place, base : base + columns, :], columns, rows)
        chosen = (slot == want).astype(BF16)
        picked = jnp.dot(chosen, normed, preferred_element_type=F32).astype(BF16)
        for j in range(columns):
            outs[j][n * CAP : (n + 1) * CAP, :] = picked[j * CAP : (j + 1) * CAP, :]


def selected(tick, places, columns, table, gain, blocks):
    width = blocks[0].shape[1]
    count = len(blocks)
    return pl.pallas_call(
        functools.partial(select_kernel, tick, places, columns),
        out_shape=[jax.ShapeDtypeStruct((count * CAP, width), BF16)] * columns,
        cost_estimate=pl.CostEstimate(
            flops=count * 10000000, bytes_accessed=count * 700000, transcendentals=0
        ),
        name="selected",
    )(table, gain, *blocks)


def ffn_kernel(columns, *refs):
    ins, (gate_ref, up_ref, down_ref) = refs[:columns], refs[columns : columns + 3]
    outs, (x_ref, acc_ref) = refs[columns + 3 : 2 * columns + 3], refs[2 * columns + 3 :]
    step, last = pl.program_id(0), pl.num_programs(0) - 1
    part_rows = ins[0].shape[0]

    @pl.when(step == 0)
    def _():
        for j in range(columns):
            x_ref[j * part_rows : (j + 1) * part_rows, :] = ins[j][...]

    x = x_ref[...]
    gate = jnp.dot(x, gate_ref[...], preferred_element_type=F32)
    upper = jnp.dot(x, up_ref[...], preferred_element_type=F32)
    hidden = (gate / (1.0 + jnp.exp(-gate)) * upper).astype(BF16)
    part = jnp.dot(hidden, down_ref[...], preferred_element_type=F32)

    @pl.when(step == 0)
    def _():
        acc_ref[...] = part

    @pl.when((step > 0) & (step < last))
    def _():
        acc_ref[...] += part

    @pl.when(step == last)
    def _():
        total = (acc_ref[...] + part).astype(BF16)
        for j in range(columns):
            outs[j][...] = total[j * part_rows : (j + 1) * part_rows, :]


def ffn(ins, gate, up, down):
    columns = len(ins)
    part_rows, width = ins[0].shape
    rows = columns * part_rows
    hidden = gate.shape[1]
    block = 256
    whole = pl.BlockSpec((part_rows, width), lambda f: (0, 0))
    return pl.pallas_call(
        functools.partial(ffn_kernel, columns),
        grid=(hidden // block,),
        in_specs=[whole] * columns
        + [
            pl.BlockSpec((width, block), lambda f: (0, f)),
            pl.BlockSpec((width, block), lambda f: (0, f)),
            pl.BlockSpec((block, width), lambda f: (f, 0)),
        ],
        out_specs=[whole] * columns,
        out_shape=[jax.ShapeDtypeStruct((part_rows, width), BF16)] * columns,
        scratch_shapes=[pltpu.VMEM((rows, width), BF16), pltpu.VMEM((rows, width), F32)],
        compiler_params=pltpu.CompilerParams(vmem_limit_bytes=32 << 20),
        cost_estimate=pl.CostEstimate(
            flops=6 * rows * width * hidden,
            bytes_accessed=6 * width * hidden + 4 * rows * width,
            transcendentals=rows * hidden,
        ),
        name="ffn",
    )(*ins, gate, up, down)


def combine_kernel(tick, places, columns, table_ref, *refs):
    backs, outs = refs[:columns], refs[columns:]
    rows = outs[0].shape[0]
    base = tick * 2 * columns
    want = (iota((columns * CAP, rows), 0) % CAP).astype(F32)
    contract = (((0,), (0,)), ((), ()))
    for n, place in enumerate(places):
        back = jnp.concatenate([ref[n * CAP : (n + 1) * CAP, :] for ref in backs], axis=0)
        slot = spread(table_ref[place, base : base + columns, :], columns, rows)
        weight = spread(table_ref[place, base + columns : base + 2 * columns, :], columns, rows)
        weight = jnp.where(slot == want, weight, 0.0)
        high = weight.astype(BF16)
        low = (weight - high.astype(F32)).astype(BF16)
        total = lax.dot_general(high, back, contract, preferred_element_type=F32)
        total += lax.dot_general(low, back, contract, preferred_element_type=F32)
        outs[n][...] = total.astype(outs[n].dtype)


def combined(tick, places, columns, table, backs, rows):
    width = backs[0].shape[1]
    count = len(places)
    return pl.pallas_call(
        functools.partial(combine_kernel, tick, places, columns),
        out_shape=[
            jax.ShapeDtypeStruct((rows, width), BF16 if abs(ORDER[place]) >= 3 else F32)
            for place in places
        ],
        cost_estimate=pl.CostEstimate(
            flops=count * 30000000, bytes_accessed=count * 700000, transcendentals=0
        ),
        name="combined",
    )(table, *backs)


def shards(state, route_ids, route_weights, norm_gain, w_gate, w_up, w_down):
    experts = lax.axis_size("expert")
    sections = lax.axis_size("pipe")
    columns = experts // RING
    ticks = route_ids.shape[0]
    rows, width = state.shape[1], state.shape[2]
    weights = (w_gate[0, 0], w_up[0, 0], w_down[0, 0])

    def move(array, dp=0, dx=0, dz=0):
        def at(p, x, z):
            return (p % sections) * experts + (x % columns) * RING + z % RING

        pairs = [
            (at(p, x, z), at(p + dp, x + dx, z + dz))
            for p in range(sections)
            for x in range(columns)
            for z in range(RING)
        ]
        return lax.ppermute(array, ("pipe", "expert"), pairs)

    own = lax.axis_index("expert")
    table = routes(route_ids[:, 0], route_weights[:, 0], experts)
    table = table.reshape(ticks * 2, columns, RING, rows).transpose(2, 0, 1, 3)
    ring_groups = [[x * RING + z for z in range(RING)] for x in range(columns)]
    table = lax.all_to_all(
        table, "expert", split_axis=0, concat_axis=0, tiled=True, axis_index_groups=ring_groups
    )
    table = table[(own % RING + jnp.array(ORDER, jnp.int32)) % RING]
    table = table[:, :, (own // RING + jnp.arange(columns, dtype=jnp.int32)) % columns]
    table = table.reshape(RING, ticks * 2 * columns, rows)

    panel = state[0]
    for tick in range(ticks):
        shift = 1 if tick else 0
        blocks = {
            -1: move(panel, shift, 0, 1),
            1: move(panel, shift, 0, -1),
            4: move(panel, shift, 0, 4),
            0: move(panel, 1, 0, 0) if shift else panel,
        }
        for k in (2, 3):
            blocks[-k] = move(blocks[-(k - 1)], 0, 0, 1)
            blocks[k] = move(blocks[k - 1], 0, 0, -1)
        parts = {}
        for group in GROUPS:
            places = tuple(ORDER.index(k) for k in group)
            sent = selected(tick, places, columns, table, norm_gain, [blocks[k] for k in group])
            ins = [sent[0]] + [move(sent[j], 0, j, 0) for j in range(1, columns)]
            outs = ffn(ins, *weights)
            backs = [outs[0]] + [move(outs[j], 0, -j, 0) for j in range(1, columns)]
            parts.update(zip(group, combined(tick, places, columns, table, backs, rows)))
        across = move(parts[4], 0, 0, 4)
        up, down = parts[3], parts[-3]
        for k in (2, 1):
            up = (move(up, 0, 0, 1).astype(F32) + parts[k]).astype(BF16)
            down = (move(down, 0, 0, -1).astype(F32) + parts[-k]).astype(BF16)
        up, down = move(up, 0, 0, 1).astype(F32), move(down, 0, 0, -1).astype(F32)
        total = parts[0] + up + down + across.astype(F32)
        panel = (blocks[0].astype(F32) + total).astype(BF16)
    return move(panel, 1, 0, 0)[None]


def solution(mesh):
    placed = (
        P("pipe", "expert", None),
        P(None, "pipe", "expert", None),
        P(None, "pipe", "expert", None),
        P("pipe", None),
        P("pipe", "expert", None, None),
        P("pipe", "expert", None, None),
        P("pipe", "expert", None, None),
    )
    return jax.shard_map(
        shards, mesh=mesh, in_specs=placed, out_specs=P("pipe", "expert", None), check_vma=False
    )
```

```python
import functools

import jax
import jax.numpy as jnp
from jax import lax
from jax.experimental import pallas as pl
from jax.experimental.pallas import tpu as pltpu
from jax.sharding import PartitionSpec as P

F32 = jnp.float32
BF16 = jnp.bfloat16
CAP = 16
RING = 8
GROUPS = ((0, 1, -1, 2, -2), (3, -3, 4))


def iota(shape, axis):
    return lax.broadcasted_iota(jnp.int32, shape, axis)


def route_kernel(columns, ids_ref, wts_ref, out_ref):
    ticks, _, rows, chosen = ids_ref.shape
    square = out_ref.shape[2]
    before = (iota((square, square), 0) < iota((square, square), 1)).astype(BF16)
    lanes = iota((rows, square), 1)
    fill = jnp.zeros((square - rows, square), F32)
    for t in range(ticks):
        ids, wts = ids_ref[t, 0], wts_ref[t, 0]
        hit = jnp.zeros((rows, square), F32)
        weight = jnp.zeros((rows, square), F32)
        for k in range(chosen):
            here = ids[:, k : k + 1] == lanes
            hit += here.astype(F32)
            weight += jnp.where(here, wts[:, k : k + 1], 0.0)
        hit = jnp.concatenate([hit, fill], axis=0).T
        weight = jnp.concatenate([weight, fill], axis=0).T
        rank = jnp.dot(hit.astype(BF16), before, preferred_element_type=F32)
        slot = jnp.where(hit > 0, rank, -1.0)
        for part, value in ((0, slot), (1, weight)):
            for x in range(columns):
                row = (t * 2 + part) * columns + x
                for z in range(RING):
                    expert = x * RING + z
                    out_ref[z, row : row + 1, :] = value[expert : expert + 1, :]


def routes(ids, wts, columns):
    ticks = ids.shape[0]
    return pl.pallas_call(
        functools.partial(route_kernel, columns),
        out_shape=jax.ShapeDtypeStruct((RING, ticks * 2 * columns, 128), F32),
        compiler_params=pltpu.CompilerParams(vmem_limit_bytes=10 << 20),
        name="routes",
    )(ids, wts)


def spread(table_ref, k, part, columns, rows):
    own = lax.axis_index("expert")
    place = lax.rem(lax.rem(own, RING) + k + RING, RING)
    parts = []
    for j in range(columns):
        row = part * columns + lax.rem(own // RING + j, columns)
        parts.append(jnp.broadcast_to(table_ref[place, pl.ds(row, 1), :][:, :rows], (CAP, rows)))
    return jnp.concatenate(parts, axis=0)


def select_kernel(places, columns, table_ref, gain_ref, *refs):
    count = len(places)
    blocks, outs = refs[:count], refs[count:]
    rows = blocks[0].shape[0]
    want = (iota((columns * CAP, rows), 0) % CAP).astype(F32)
    for n, place in enumerate(places):
        wide = blocks[n][...].astype(F32)
        scale = lax.rsqrt(jnp.mean(wide * wide, axis=-1, keepdims=True) + 1e-06)
        normed = (wide * scale * gain_ref[...]).astype(BF16)
        slot = spread(table_ref, place, 0, columns, rows)
        chosen = (slot == want).astype(BF16)
        picked = jnp.dot(chosen, normed, preferred_element_type=F32).astype(BF16)
        for j in range(columns):
            outs[j][n * CAP : (n + 1) * CAP, :] = picked[j * CAP : (j + 1) * CAP, :]


def selected(places, columns, table, gain, blocks):
    width = blocks[0].shape[1]
    count = len(blocks)
    return pl.pallas_call(
        functools.partial(select_kernel, places, columns),
        out_shape=[jax.ShapeDtypeStruct((count * CAP, width), BF16)] * columns,
        compiler_params=pltpu.CompilerParams(vmem_limit_bytes=10 << 20),
        cost_estimate=pl.CostEstimate(
            flops=count * 10000000, bytes_accessed=count * 700000, transcendentals=0
        ),
        name="selected",
    )(table, gain, *blocks)


def ffn_kernel(columns, *refs):
    ins, (gate_ref, up_ref, down_ref) = refs[:columns], refs[columns : columns + 3]
    outs, (x_ref, acc_ref) = refs[columns + 3 : 2 * columns + 3], refs[2 * columns + 3 :]
    step, last = pl.program_id(0), pl.num_programs(0) - 1
    part_rows = ins[0].shape[0]

    @pl.when(step == 0)
    def _():
        for j in range(columns):
            x_ref[j * part_rows : (j + 1) * part_rows, :] = ins[j][...]

    x = x_ref[...]
    gate = jnp.dot(x, gate_ref[...], preferred_element_type=F32)
    upper = jnp.dot(x, up_ref[...], preferred_element_type=F32)
    hidden = (gate / (1.0 + jnp.exp(-gate)) * upper).astype(BF16)
    part = jnp.dot(hidden, down_ref[...], preferred_element_type=F32)

    @pl.when(step == 0)
    def _():
        acc_ref[...] = part

    @pl.when((step > 0) & (step < last))
    def _():
        acc_ref[...] += part

    @pl.when(step == last)
    def _():
        total = (acc_ref[...] + part).astype(BF16)
        for j in range(columns):
            outs[j][...] = total[j * part_rows : (j + 1) * part_rows, :]


def ffn(ins, gate, up, down):
    columns = len(ins)
    part_rows, width = ins[0].shape
    rows = columns * part_rows
    hidden = gate.shape[1]
    block = 256
    whole = pl.BlockSpec((part_rows, width), lambda f: (0, 0))
    return pl.pallas_call(
        functools.partial(ffn_kernel, columns),
        grid=(hidden // block,),
        in_specs=[whole] * columns
        + [
            pl.BlockSpec((width, block), lambda f: (0, f)),
            pl.BlockSpec((width, block), lambda f: (0, f)),
            pl.BlockSpec((block, width), lambda f: (f, 0)),
        ],
        out_specs=[whole] * columns,
        out_shape=[jax.ShapeDtypeStruct((part_rows, width), BF16)] * columns,
        scratch_shapes=[pltpu.VMEM((rows, width), BF16), pltpu.VMEM((rows, width), F32)],
        compiler_params=pltpu.CompilerParams(vmem_limit_bytes=24 << 20),
        cost_estimate=pl.CostEstimate(
            flops=6 * rows * width * hidden,
            bytes_accessed=6 * width * hidden + 4 * rows * width,
            transcendentals=rows * hidden,
        ),
        name="ffn",
    )(*ins, gate, up, down)


def combine_kernel(places, columns, table_ref, *refs):
    backs, outs = refs[:columns], refs[columns:]
    rows = outs[0].shape[0]
    want = (iota((columns * CAP, rows), 0) % CAP).astype(F32)
    contract = (((0,), (0,)), ((), ()))
    for n, place in enumerate(places):
        back = jnp.concatenate([ref[n * CAP : (n + 1) * CAP, :] for ref in backs], axis=0)
        slot = spread(table_ref, place, 0, columns, rows)
        weight = spread(table_ref, place, 1, columns, rows)
        weight = jnp.where(slot == want, weight, 0.0)
        high = weight.astype(BF16)
        low = (weight - high.astype(F32)).astype(BF16)
        total = lax.dot_general(high, back, contract, preferred_element_type=F32)
        total += lax.dot_general(low, back, contract, preferred_element_type=F32)
        outs[n][...] = total.astype(outs[n].dtype)


def combined(places, columns, table, backs, rows):
    width = backs[0].shape[1]
    count = len(places)
    return pl.pallas_call(
        functools.partial(combine_kernel, places, columns),
        out_shape=[
            jax.ShapeDtypeStruct((rows, width), BF16 if abs(place) >= 3 else F32)
            for place in places
        ],
        compiler_params=pltpu.CompilerParams(vmem_limit_bytes=10 << 20),
        cost_estimate=pl.CostEstimate(
            flops=count * 30000000, bytes_accessed=count * 700000, transcendentals=0
        ),
        name="combined",
    )(table, *backs)


def shards(state, route_ids, route_weights, norm_gain, w_gate, w_up, w_down):
    experts = lax.axis_size("expert")
    sections = lax.axis_size("pipe")
    columns = experts // RING
    ticks = route_ids.shape[0]
    rows, width = state.shape[1], state.shape[2]
    weights = (w_gate[0, 0], w_up[0, 0], w_down[0, 0])

    def move(array, dp=0, dx=0, dz=0):
        def at(p, x, z):
            return (p % sections) * experts + (x % columns) * RING + z % RING

        pairs = [
            (at(p, x, z), at(p + dp, x + dx, z + dz))
            for p in range(sections)
            for x in range(columns)
            for z in range(RING)
        ]
        return lax.ppermute(array, ("pipe", "expert"), pairs)

    table = routes(route_ids, route_weights, columns)
    ring_groups = [[x * RING + z for z in range(RING)] for x in range(columns)]
    table = lax.all_to_all(
        table, "expert", split_axis=0, concat_axis=0, tiled=True, axis_index_groups=ring_groups
    )
    table = table.reshape(RING, ticks, 2 * columns, 128)

    def tick_step(tick, panel):
        here = lax.dynamic_index_in_dim(table, tick, axis=1, keepdims=False)

        def select(group):
            return list(selected(group, columns, here, norm_gain, [blocks[k] for k in group]))

        def cross(arrays, sign):
            return [arrays[0]] + [move(arrays[j], 0, sign * j, 0) for j in range(1, columns)]

        def combine(group, backs):
            return dict(zip(group, combined(group, columns, here, backs, rows)))

        blocks = {-1: move(panel, 1, 0, 1), 1: move(panel, 1, 0, -1), 0: move(panel, 1, 0, 0)}
        for k in (1, 2):
            blocks[-k - 1] = move(blocks[-k], 0, 0, 1)
            blocks[k + 1] = move(blocks[k], 0, 0, -1)
        blocks[4] = move(blocks[3], 0, 0, -1)
        parts = {}
        for group in GROUPS:
            outs = ffn(cross(select(group), 1), *weights)
            parts |= combine(group, cross(outs, -1))
        up = (move(parts[4], 0, 0, 1).astype(F32) + parts[3].astype(F32)).astype(BF16)
        down = parts[-3]
        for k in (2, 1):
            up = (move(up, 0, 0, 1).astype(F32) + parts[k]).astype(BF16)
            down = (move(down, 0, 0, -1).astype(F32) + parts[-k]).astype(BF16)
        up, down = move(up, 0, 0, 1).astype(F32), move(down, 0, 0, -1).astype(F32)
        total = parts[0] + up + down
        return (blocks[0].astype(F32) + total).astype(BF16)

    panel = lax.fori_loop(0, ticks, tick_step, move(state[0], -1, 0, 0))
    return move(panel, 1, 0, 0)[None]


def solution(mesh):
    placed = (
        P("pipe", "expert", None),
        P(None, "pipe", "expert", None),
        P(None, "pipe", "expert", None),
        P("pipe", None),
        P("pipe", "expert", None, None),
        P("pipe", "expert", None, None),
        P("pipe", "expert", None, None),
    )
    return jax.shard_map(
        shards, mesh=mesh, in_specs=placed, out_specs=P("pipe", "expert", None), check_vma=False
    )
```

```python
import functools

import jax
import jax.numpy as jnp
from jax import lax
from jax.experimental import pallas as pl
from jax.experimental.pallas import tpu as pltpu
from jax.sharding import PartitionSpec as P

F32 = jnp.float32
BF16 = jnp.bfloat16
CAP = 16
RING = 8
GROUPS = ((0, 1, -1, 2, -2), (3, -3, 4))


def iota(shape, axis):
    return lax.broadcasted_iota(jnp.int32, shape, axis)


def route_kernel(columns, ids_ref, wts_ref, out_ref):
    ticks, _, rows, chosen = ids_ref.shape
    square = out_ref.shape[2]
    before = (iota((square, square), 0) < iota((square, square), 1)).astype(BF16)
    lanes = iota((rows, square), 1)
    fill = jnp.zeros((square - rows, square), F32)
    for t in range(ticks):
        ids, wts = ids_ref[t, 0], wts_ref[t, 0]
        hit = jnp.zeros((rows, square), F32)
        weight = jnp.zeros((rows, square), F32)
        for k in range(chosen):
            here = ids[:, k : k + 1] == lanes
            hit += here.astype(F32)
            weight += jnp.where(here, wts[:, k : k + 1], 0.0)
        hit = jnp.concatenate([hit, fill], axis=0).T
        weight = jnp.concatenate([weight, fill], axis=0).T
        rank = jnp.dot(hit.astype(BF16), before, preferred_element_type=F32)
        slot = jnp.where(hit > 0, rank, -1.0)
        for part, value in ((0, slot), (1, weight)):
            for x in range(columns):
                row = (t * 2 + part) * columns + x
                for z in range(RING):
                    expert = x * RING + z
                    out_ref[z, row : row + 1, :] = value[expert : expert + 1, :]


def routes(ids, wts, columns):
    ticks = ids.shape[0]
    return pl.pallas_call(
        functools.partial(route_kernel, columns),
        out_shape=jax.ShapeDtypeStruct((RING, ticks * 2 * columns, 128), F32),
        compiler_params=pltpu.CompilerParams(vmem_limit_bytes=10 << 20),
        name="routes",
    )(ids, wts)


def spread(table_ref, k, part, columns, rows):
    own = lax.axis_index("expert")
    place = lax.rem(lax.rem(own, RING) + k + RING, RING)
    parts = []
    for j in range(columns):
        row = part * columns + lax.rem(own // RING + j, columns)
        parts.append(jnp.broadcast_to(table_ref[place, pl.ds(row, 1), :][:, :rows], (CAP, rows)))
    return jnp.concatenate(parts, axis=0)


def select_kernel(places, columns, table_ref, gain_ref, *refs):
    count = len(places)
    blocks, outs = refs[:count], refs[count:]
    rows = blocks[0].shape[0]
    want = (iota((columns * CAP, rows), 0) % CAP).astype(F32)
    for n, place in enumerate(places):
        wide = blocks[n][...].astype(F32)
        scale = lax.rsqrt(jnp.mean(wide * wide, axis=-1, keepdims=True) + 1e-06)
        normed = (wide * scale * gain_ref[...]).astype(BF16)
        slot = spread(table_ref, place, 0, columns, rows)
        chosen = (slot == want).astype(BF16)
        picked = jnp.dot(chosen, normed, preferred_element_type=F32).astype(BF16)
        for j in range(columns):
            outs[j][n * CAP : (n + 1) * CAP, :] = picked[j * CAP : (j + 1) * CAP, :]


def selected(places, columns, table, gain, blocks):
    width = blocks[0].shape[1]
    count = len(blocks)
    return pl.pallas_call(
        functools.partial(select_kernel, places, columns),
        out_shape=[jax.ShapeDtypeStruct((count * CAP, width), BF16)] * columns,
        compiler_params=pltpu.CompilerParams(vmem_limit_bytes=10 << 20),
        cost_estimate=pl.CostEstimate(
            flops=count * 10000000, bytes_accessed=count * 700000, transcendentals=0
        ),
        name="selected",
    )(table, gain, *blocks)


def ffn_kernel(columns, *refs):
    ins, (gate_ref, up_ref, down_ref) = refs[:columns], refs[columns : columns + 3]
    outs, (x_ref, acc_ref) = refs[columns + 3 : 2 * columns + 3], refs[2 * columns + 3 :]
    step, last = pl.program_id(0), pl.num_programs(0) - 1
    part_rows = ins[0].shape[0]

    @pl.when(step == 0)
    def _():
        for j in range(columns):
            x_ref[j * part_rows : (j + 1) * part_rows, :] = ins[j][...]

    x = x_ref[...]
    gate = jnp.dot(x, gate_ref[...], preferred_element_type=F32)
    upper = jnp.dot(x, up_ref[...], preferred_element_type=F32)
    hidden = (gate / (1.0 + jnp.exp(-gate)) * upper).astype(BF16)
    part = jnp.dot(hidden, down_ref[...], preferred_element_type=F32)

    @pl.when(step == 0)
    def _():
        acc_ref[...] = part

    @pl.when((step > 0) & (step < last))
    def _():
        acc_ref[...] += part

    @pl.when(step == last)
    def _():
        total = (acc_ref[...] + part).astype(BF16)
        for j in range(columns):
            outs[j][...] = total[j * part_rows : (j + 1) * part_rows, :]


def ffn(ins, gate, up, down):
    columns = len(ins)
    part_rows, width = ins[0].shape
    rows = columns * part_rows
    hidden = gate.shape[1]
    block = 256
    whole = pl.BlockSpec((part_rows, width), lambda f: (0, 0))
    return pl.pallas_call(
        functools.partial(ffn_kernel, columns),
        grid=(hidden // block,),
        in_specs=[whole] * columns
        + [
            pl.BlockSpec((width, block), lambda f: (0, f)),
            pl.BlockSpec((width, block), lambda f: (0, f)),
            pl.BlockSpec((block, width), lambda f: (f, 0)),
        ],
        out_specs=[whole] * columns,
        out_shape=[jax.ShapeDtypeStruct((part_rows, width), BF16)] * columns,
        scratch_shapes=[pltpu.VMEM((rows, width), BF16), pltpu.VMEM((rows, width), F32)],
        compiler_params=pltpu.CompilerParams(vmem_limit_bytes=24 << 20),
        cost_estimate=pl.CostEstimate(
            flops=6 * rows * width * hidden,
            bytes_accessed=6 * width * hidden + 4 * rows * width,
            transcendentals=rows * hidden,
        ),
        name="ffn",
    )(*ins, gate, up, down)


def combine_kernel(places, columns, table_ref, *refs):
    backs, outs = refs[:columns], refs[columns:]
    rows = outs[0].shape[0]
    want = (iota((columns * CAP, rows), 0) % CAP).astype(F32)
    contract = (((0,), (0,)), ((), ()))
    for n, place in enumerate(places):
        back = jnp.concatenate([ref[n * CAP : (n + 1) * CAP, :] for ref in backs], axis=0)
        slot = spread(table_ref, place, 0, columns, rows)
        weight = spread(table_ref, place, 1, columns, rows)
        weight = jnp.where(slot == want, weight, 0.0)
        high = weight.astype(BF16)
        low = (weight - high.astype(F32)).astype(BF16)
        total = lax.dot_general(high, back, contract, preferred_element_type=F32)
        total += lax.dot_general(low, back, contract, preferred_element_type=F32)
        outs[n][...] = total.astype(outs[n].dtype)


def combined(places, columns, table, backs, rows):
    width = backs[0].shape[1]
    count = len(places)
    return pl.pallas_call(
        functools.partial(combine_kernel, places, columns),
        out_shape=[
            jax.ShapeDtypeStruct((rows, width), BF16 if abs(place) >= 3 else F32)
            for place in places
        ],
        compiler_params=pltpu.CompilerParams(vmem_limit_bytes=10 << 20),
        cost_estimate=pl.CostEstimate(
            flops=count * 30000000, bytes_accessed=count * 700000, transcendentals=0
        ),
        name="combined",
    )(table, *backs)


def shards(state, route_ids, route_weights, norm_gain, w_gate, w_up, w_down):
    experts = lax.axis_size("expert")
    sections = lax.axis_size("pipe")
    columns = experts // RING
    ticks = route_ids.shape[0]
    rows, width = state.shape[1], state.shape[2]
    weights = tuple(
        pltpu.with_memory_space_constraint(w[0, 0], pltpu.HBM) for w in (w_gate, w_up, w_down)
    )

    def move(array, dp=0, dx=0, dz=0):
        def at(p, x, z):
            return (p % sections) * experts + (x % columns) * RING + z % RING

        pairs = [
            (at(p, x, z), at(p + dp, x + dx, z + dz))
            for p in range(sections)
            for x in range(columns)
            for z in range(RING)
        ]
        return lax.ppermute(array, ("pipe", "expert"), pairs)

    table = routes(route_ids, route_weights, columns)
    ring_groups = [[x * RING + z for z in range(RING)] for x in range(columns)]
    table = lax.all_to_all(
        table, "expert", split_axis=0, concat_axis=0, tiled=True, axis_index_groups=ring_groups
    )
    table = table.reshape(RING, ticks, 2 * columns, 128)

    def tick_step(tick, panel):
        here = lax.dynamic_index_in_dim(table, tick, axis=1, keepdims=False)

        def select(group):
            return list(selected(group, columns, here, norm_gain, [blocks[k] for k in group]))

        def cross(arrays, sign):
            return [arrays[0]] + [move(arrays[j], 0, sign * j, 0) for j in range(1, columns)]

        def combine(group, backs):
            return dict(zip(group, combined(group, columns, here, backs, rows)))

        blocks = {0: panel, -1: move(panel, 0, 0, 1), 1: move(panel, 0, 0, -1)}
        for k in (1, 2):
            blocks[-k - 1] = move(blocks[-k], 0, 0, 1)
            blocks[k + 1] = move(blocks[k], 0, 0, -1)
        blocks[4] = move(blocks[3], 0, 0, -1)
        parts = {}
        for group in GROUPS:
            outs = ffn(cross(select(group), 1), *weights)
            parts |= combine(group, cross(outs, -1))
        up = (move(parts[4], 0, 0, 1).astype(F32) + parts[3].astype(F32)).astype(BF16)
        down = parts[-3]
        for k in (2, 1):
            up = (move(up, 0, 0, 1).astype(F32) + parts[k]).astype(BF16)
            down = (move(down, 0, 0, -1).astype(F32) + parts[-k]).astype(BF16)
        kept = move(panel.astype(F32) + parts[0], 1, 0, 0)
        up, down = move(up, 1, 0, 1).astype(F32), move(down, 1, 0, -1).astype(F32)
        return (kept + (up + down)).astype(BF16)

    return lax.fori_loop(0, ticks, tick_step, state[0])[None]


def solution(mesh):
    placed = (
        P("pipe", "expert", None),
        P(None, "pipe", "expert", None),
        P(None, "pipe", "expert", None),
        P("pipe", None),
        P("pipe", "expert", None, None),
        P("pipe", "expert", None, None),
        P("pipe", "expert", None, None),
    )
    return jax.shard_map(
        shards, mesh=mesh, in_specs=placed, out_specs=P("pipe", "expert", None), check_vma=False
    )
```

```python
import functools

import jax
import jax.numpy as jnp
from jax import lax
from jax.experimental import pallas as pl
from jax.experimental.pallas import tpu as pltpu
from jax.sharding import PartitionSpec as P

F32 = jnp.float32
BF16 = jnp.bfloat16
CAP = 16
RING = 8
GROUPS = ((0, 1, -1, 2, -2), (3, -3, 4))


def iota(shape, axis):
    return lax.broadcasted_iota(jnp.int32, shape, axis)


def route_kernel(columns, ids_ref, wts_ref, out_ref):
    ticks, _, rows, chosen = ids_ref.shape
    square = out_ref.shape[2]
    before = (iota((square, square), 0) < iota((square, square), 1)).astype(BF16)
    lanes = iota((rows, square), 1)
    fill = jnp.zeros((square - rows, square), F32)
    for t in range(ticks):
        ids, wts = ids_ref[t, 0], wts_ref[t, 0]
        hit = jnp.zeros((rows, square), F32)
        weight = jnp.zeros((rows, square), F32)
        for k in range(chosen):
            here = ids[:, k : k + 1] == lanes
            hit += here.astype(F32)
            weight += jnp.where(here, wts[:, k : k + 1], 0.0)
        hit = jnp.concatenate([hit, fill], axis=0).T
        weight = jnp.concatenate([weight, fill], axis=0).T
        rank = jnp.dot(hit.astype(BF16), before, preferred_element_type=F32)
        slot = jnp.where(hit > 0, rank, -1.0)
        for part, value in ((0, slot), (1, weight)):
            for x in range(columns):
                row = (t * 2 + part) * columns + x
                for z in range(RING):
                    expert = x * RING + z
                    out_ref[z, row : row + 1, :] = value[expert : expert + 1, :]


def routes(ids, wts, columns):
    ticks = ids.shape[0]
    return pl.pallas_call(
        functools.partial(route_kernel, columns),
        out_shape=jax.ShapeDtypeStruct((RING, ticks * 2 * columns, 128), F32),
        compiler_params=pltpu.CompilerParams(vmem_limit_bytes=10 << 20),
        name="routes",
    )(ids, wts)


def spread(table_ref, k, part, columns, rows):
    own = lax.axis_index("expert")
    place = lax.rem(lax.rem(own, RING) + k + RING, RING)
    parts = []
    for j in range(columns):
        row = part * columns + lax.rem(own // RING + j, columns)
        parts.append(jnp.broadcast_to(table_ref[place, pl.ds(row, 1), :][:, :rows], (CAP, rows)))
    return jnp.concatenate(parts, axis=0)


def select_kernel(places, columns, table_ref, gain_ref, *refs):
    count = len(places)
    blocks, outs = refs[:count], refs[count:]
    rows = blocks[0].shape[0]
    want = (iota((columns * CAP, rows), 0) % CAP).astype(F32)
    for n, place in enumerate(places):
        wide = blocks[n][...].astype(F32)
        scale = lax.rsqrt(jnp.mean(wide * wide, axis=-1, keepdims=True) + 1e-06)
        normed = (wide * scale * gain_ref[...]).astype(BF16)
        slot = spread(table_ref, place, 0, columns, rows)
        chosen = (slot == want).astype(BF16)
        picked = jnp.dot(chosen, normed, preferred_element_type=F32).astype(BF16)
        for j in range(columns):
            outs[j][n * CAP : (n + 1) * CAP, :] = picked[j * CAP : (j + 1) * CAP, :]


def selected(places, columns, table, gain, blocks):
    width = blocks[0].shape[1]
    count = len(blocks)
    return pl.pallas_call(
        functools.partial(select_kernel, places, columns),
        out_shape=[jax.ShapeDtypeStruct((count * CAP, width), BF16)] * columns,
        compiler_params=pltpu.CompilerParams(vmem_limit_bytes=10 << 20),
        cost_estimate=pl.CostEstimate(
            flops=count * 10000000, bytes_accessed=count * 700000, transcendentals=0
        ),
        name="selected",
    )(table, gain, *blocks)


def ffn_kernel(columns, depth_steps, *refs):
    ins, (gate_ref, up_ref, down_ref) = refs[:columns], refs[columns : columns + 3]
    outs = refs[columns + 3 : 2 * columns + 3]
    gate_acc, up_acc, hidden_ref, acc_ref = refs[2 * columns + 3 :]
    step = pl.program_id(0)
    part_rows = outs[0].shape[0]
    half = down_ref.shape[0]

    @pl.when(step < depth_steps)
    def _():
        x = jnp.concatenate([ref[...] for ref in ins], axis=0)
        gate = jnp.dot(x, gate_ref[...], preferred_element_type=F32)
        upper = jnp.dot(x, up_ref[...], preferred_element_type=F32)

        @pl.when(step == 0)
        def _():
            gate_acc[...] = gate
            up_acc[...] = upper

        @pl.when(step > 0)
        def _():
            gate_acc[...] += gate
            up_acc[...] += upper

    @pl.when(step == depth_steps)
    def _():
        gate = gate_acc[...]
        hidden_ref[...] = (gate / (1.0 + jnp.exp(-gate)) * up_acc[...]).astype(BF16)
        acc_ref[...] = jnp.dot(hidden_ref[:, :half], down_ref[...], preferred_element_type=F32)

    @pl.when(step == depth_steps + 1)
    def _():
        part = jnp.dot(hidden_ref[:, half:], down_ref[...], preferred_element_type=F32)
        total = (acc_ref[...] + part).astype(BF16)
        for j in range(columns):
            outs[j][...] = total[j * part_rows : (j + 1) * part_rows, :]


def ffn(ins, gate, up, down):
    columns = len(ins)
    part_rows, width = ins[0].shape
    rows = columns * part_rows
    hidden = gate.shape[1]
    depth_steps = 2
    depth = width // depth_steps
    half = hidden // 2
    last = depth_steps - 1
    whole = pl.BlockSpec((part_rows, width), lambda f: (0, 0))
    return pl.pallas_call(
        functools.partial(ffn_kernel, columns, depth_steps),
        grid=(depth_steps + 2,),
        in_specs=[pl.BlockSpec((part_rows, depth), lambda f: (0, jnp.minimum(f, last)))] * columns
        + [
            pl.BlockSpec((depth, hidden), lambda f: (jnp.minimum(f, last), 0)),
            pl.BlockSpec((depth, hidden), lambda f: (jnp.minimum(f, last), 0)),
            pl.BlockSpec((half, width), lambda f: (jnp.maximum(f - depth_steps, 0), 0)),
        ],
        out_specs=[whole] * columns,
        out_shape=[jax.ShapeDtypeStruct((part_rows, width), BF16)] * columns,
        scratch_shapes=[
            pltpu.VMEM((rows, hidden), F32),
            pltpu.VMEM((rows, hidden), F32),
            pltpu.VMEM((rows, hidden), BF16),
            pltpu.VMEM((rows, width), F32),
        ],
        compiler_params=pltpu.CompilerParams(vmem_limit_bytes=24 << 20),
        cost_estimate=pl.CostEstimate(
            flops=6 * rows * width * hidden,
            bytes_accessed=6 * width * hidden + 4 * rows * width,
            transcendentals=rows * hidden,
        ),
        name="ffn",
    )(*ins, gate, up, down)


def combine_kernel(places, columns, table_ref, *refs):
    backs, outs = refs[:columns], refs[columns:]
    rows = outs[0].shape[0]
    want = (iota((columns * CAP, rows), 0) % CAP).astype(F32)
    contract = (((0,), (0,)), ((), ()))
    for n, place in enumerate(places):
        back = jnp.concatenate([ref[n * CAP : (n + 1) * CAP, :] for ref in backs], axis=0)
        slot = spread(table_ref, place, 0, columns, rows)
        weight = spread(table_ref, place, 1, columns, rows)
        weight = jnp.where(slot == want, weight, 0.0)
        high = weight.astype(BF16)
        low = (weight - high.astype(F32)).astype(BF16)
        total = lax.dot_general(high, back, contract, preferred_element_type=F32)
        total += lax.dot_general(low, back, contract, preferred_element_type=F32)
        outs[n][...] = total.astype(outs[n].dtype)


def combined(places, columns, table, backs, rows):
    width = backs[0].shape[1]
    count = len(places)
    return pl.pallas_call(
        functools.partial(combine_kernel, places, columns),
        out_shape=[
            jax.ShapeDtypeStruct((rows, width), BF16 if abs(place) >= 3 else F32)
            for place in places
        ],
        compiler_params=pltpu.CompilerParams(vmem_limit_bytes=10 << 20),
        cost_estimate=pl.CostEstimate(
            flops=count * 30000000, bytes_accessed=count * 700000, transcendentals=0
        ),
        name="combined",
    )(table, *backs)


def shards(state, route_ids, route_weights, norm_gain, w_gate, w_up, w_down):
    experts = lax.axis_size("expert")
    sections = lax.axis_size("pipe")
    columns = experts // RING
    ticks = route_ids.shape[0]
    rows, width = state.shape[1], state.shape[2]
    weights = tuple(
        pltpu.with_memory_space_constraint(w[0, 0], pltpu.HBM) for w in (w_gate, w_up, w_down)
    )

    def move(array, dp=0, dx=0, dz=0):
        def at(p, x, z):
            return (p % sections) * experts + (x % columns) * RING + z % RING

        pairs = [
            (at(p, x, z), at(p + dp, x + dx, z + dz))
            for p in range(sections)
            for x in range(columns)
            for z in range(RING)
        ]
        return lax.ppermute(array, ("pipe", "expert"), pairs)

    table = routes(route_ids, route_weights, columns)
    ring_groups = [[x * RING + z for z in range(RING)] for x in range(columns)]
    table = lax.all_to_all(
        table, "expert", split_axis=0, concat_axis=0, tiled=True, axis_index_groups=ring_groups
    )
    table = table.reshape(RING, ticks, 2 * columns, 128)

    def tick_step(tick, panel):
        here = lax.dynamic_index_in_dim(table, tick, axis=1, keepdims=False)

        def select(group):
            return list(selected(group, columns, here, norm_gain, [blocks[k] for k in group]))

        def cross(arrays, sign):
            return [arrays[0]] + [move(arrays[j], 0, sign * j, 0) for j in range(1, columns)]

        def combine(group, backs):
            return dict(zip(group, combined(group, columns, here, backs, rows)))

        blocks = {0: panel, -1: move(panel, 0, 0, 1), 1: move(panel, 0, 0, -1)}
        for k in (1, 2):
            blocks[-k - 1] = move(blocks[-k], 0, 0, 1)
            blocks[k + 1] = move(blocks[k], 0, 0, -1)
        blocks[4] = move(blocks[3], 0, 0, -1)
        parts = {}
        for group in GROUPS:
            outs = ffn(cross(select(group), 1), *weights)
            parts |= combine(group, cross(outs, -1))
        up = (move(parts[4], 0, 0, 1).astype(F32) + parts[3].astype(F32)).astype(BF16)
        down = parts[-3]
        for k in (2, 1):
            up = (move(up, 0, 0, 1).astype(F32) + parts[k]).astype(BF16)
            down = (move(down, 0, 0, -1).astype(F32) + parts[-k]).astype(BF16)
        kept = move(panel.astype(F32) + parts[0], 1, 0, 0)
        up, down = move(up, 1, 0, 1).astype(F32), move(down, 1, 0, -1).astype(F32)
        return (kept + (up + down)).astype(BF16)

    return lax.fori_loop(0, ticks, tick_step, state[0])[None]


def solution(mesh):
    placed = (
        P("pipe", "expert", None),
        P(None, "pipe", "expert", None),
        P(None, "pipe", "expert", None),
        P("pipe", None),
        P("pipe", "expert", None, None),
        P("pipe", "expert", None, None),
        P("pipe", "expert", None, None),
    )
    return jax.shard_map(
        shards, mesh=mesh, in_specs=placed, out_specs=P("pipe", "expert", None), check_vma=False
    )
```
